256 devices in a mesh: rep: 32 (over z, y_lo, core), tp: 8 (over x, y_hi).
Axes of the slice: x: 4, y: 4 (y_hi: 2, y_lo: 2; y = y_hi * 2 + y_lo), z: 8, core: 2. Of those that a mesh axis runs over, the one named last changes fastest.
Arguments:
- context: bfloat16 [8192, 3072], P('rep', 'tp'), may hold values from -6 to 6
- residual: bfloat16 [8192, 5120], P(('rep', 'tp')), may hold values from -6 to 6
- cotangent: bfloat16 [8192, 5120], P(('rep', 'tp')), may hold values from -6 to 6
- numer: bfloat16 [32, 3072, 5120], P('rep', 'tp'), may hold values from -0.109375 to 0.109375
- weight: float32 [32], P('rep'), may hold values from 0.5 to 2
- step: int32 [1], replicated, may hold values from 0 to 999999
Outputs:
- output: bfloat16 [8192, 5120], P(('rep', 'tp'))
- grad_context: bfloat16 [8192, 3072], P('rep', 'tp')
- numer_next: bfloat16 [32, 3072, 5120], P('rep', 'tp')
- weight_next: float32 [32], P('rep')
The draws below stay inside these ranges and needn't reach their ends.
All inputs are finite; a program needn't handle non-finite values.
Results may differ from the reference program's by a relative error of at most 0.013.
Values may be sent and summed in bfloat16 or wider, within the bound.
A program may use at most 192 MiB of HBM per device.

```python
import math
import jax
import jax.numpy as jnp
from jax import lax

D = 5120
TOK = 256
PEER_BITS = 3
HH = 3072
REPS = 32
TOKENS = 8192


def shard_levels(stream_key, shape, shards, low, high):
    def one(axis_at, blocks):
        heights = jax.random.uniform(jax.random.fold_in(jax.random.fold_in(stream_key, 6), axis_at), (blocks,), jnp.float32, low / len(shards), high / len(shards))
        return jnp.repeat(jnp.exp(heights), shape[axis_at] // blocks).reshape((-1,) + (1,) * (len(shape) - axis_at - 1))

    loudness = one(*shards[0])
    for cut in shards[1:]:
        loudness = loudness * one(*cut)
    return loudness


def noise(own_key, extent, deviation, bound, shards=(), held_as=jnp.bfloat16):
    values = deviation * jax.random.normal(own_key, extent, jnp.float32)
    if shards:
        values = values * shard_levels(own_key, extent, shards, -0.22, 0.18)
    return jnp.clip(values, -bound, bound).astype(held_as)


def setup_inputs(seed: int = 0) -> dict:
    splits = jax.random.split(jax.random.key(seed), 7)
    return {
        "context": noise(splits[0], (TOKENS, HH), 1.0, 6.0, ((0, 32), (1, 8))),
        "residual": noise(splits[1], (TOKENS, D), 1.0, 6.0, ((0, 256),)),
        "cotangent": noise(splits[2], (TOKENS, D), 1.0, 6.0, ((0, 256),)),
        "numer": noise(splits[3], (REPS, HH, D), HH ** -0.5, 0.109375, ((0, 32), (1, 8))),
        "weight": jnp.clip(jnp.exp(math.log(2.0) - 1.3862944 * jax.random.uniform(splits[4], (REPS,), jnp.float32) ** shard_levels(splits[4], (REPS,), ((0, 32),), -0.2, 0.2)), 0.5, 2.0),
        "step": jax.random.randint(splits[5], (1,), 0, 1000000).astype(jnp.int32),
    }


LEARN = 0.001


def one_replica(items):
    ctx, resid, cot, numer_r, weight_r, peer_numer = items
    params = (numer_r.astype(jnp.float32) / weight_r).astype(jnp.bfloat16)
    projected = jnp.dot(ctx, params, preferred_element_type=jnp.float32)
    output = (resid.astype(jnp.float32) + projected).astype(jnp.bfloat16)
    grad_ctx = lax.dot_general(cot, params, (((1,), (1,)), ((), ())), preferred_element_type=jnp.float32).astype(jnp.bfloat16)
    grad_params = lax.dot_general(ctx, cot, (((0,), (0,)), ((), ())), preferred_element_type=jnp.float32)
    mixed = 0.5 * (numer_r.astype(jnp.float32) + peer_numer.astype(jnp.float32)) - LEARN * grad_params
    return output, grad_ctx, mixed.astype(jnp.bfloat16)


def reference(context, residual, cotangent, numer, weight, step):
    exponent = jnp.remainder(step[0].astype(jnp.int32), jnp.int32(PEER_BITS + 1)).astype(jnp.int32)
    distance = jnp.left_shift(jnp.int32(1), exponent)
    peer_numer = jnp.roll(numer, distance, axis=0)
    peer_weight = jnp.roll(weight, distance, axis=0)
    ctx = context.reshape(REPS, TOK, HH)
    resid = residual.reshape(REPS, TOK, D)
    cot = cotangent.reshape(REPS, TOK, D)
    output, grad_ctx, numer_next = lax.map(one_replica, (ctx, resid, cot, numer, weight, peer_numer))
    weight_next = 0.5 * (weight + peer_weight)
    return output.reshape(TOKENS, D), grad_ctx.reshape(TOKENS, HH), numer_next, weight_next
```

```python
import functools

import jax
import jax.numpy as jnp
from jax import lax
from jax.experimental import pallas as pl
from jax.experimental.pallas import tpu as pltpu
from jax.sharding import PartitionSpec as P

PEER_BITS = 3
LEARN = 0.001
MESH = pl.DeviceIdType.MESH
WIDE = 256
FLAT = 1024

PLANS = (
    (((1,), 32, 12),),
    (((2,), 32, 12),),
    (((-12, -12, -4), 16, 2), ((4,), 32, 11)),
    (((-12, -12), 16, 6), ((8,), 32, 9)),
)
EARLY = (5, 5, 13, 15)


def pieces_of(k):
    row, pieces = 0, []
    for legs, rows, count in PLANS[k]:
        for _ in range(count):
            pieces.append((row, rows, legs))
            row += rows
    return row, pieces


def kernel(k, reps, tps, names, *refs):
    r = dict(zip(names, refs, strict=True))
    rep, tp = lax.axis_index("rep"), lax.axis_index("tp")
    x, y_hi = tp // 2, tp % 2
    over = rep + 2 - 4 * ((rep // 2) % 2)
    flip = tp + 1 - 2 * y_hi
    ahead, behind = (tp + 2) % tps, (tp + tps - 2) % tps
    at = lambda a, b: {"rep": a, "tp": b}
    _, pieces = pieces_of(k)
    feats, wide = r["numer"].shape
    toks = r["cot"].shape[0]

    used = {"s": 0, "r": 0}
    sends = []

    def send(src, dst, where):
        i = used["s"]
        used["s"] += 1
        copy = pltpu.make_async_remote_copy(
            src_ref=src,
            dst_ref=dst,
            send_sem=r["ss"].at[i],
            recv_sem=r["rs"].at[i],
            device_id=where,
            device_id_type=MESH,
        )
        copy.start()
        sends.append(copy)
        return copy

    def local(src, dst):
        i = used["r"]
        used["r"] += 1
        copy = pltpu.make_async_copy(src, dst, r["ls"].at[i])
        copy.start()
        return copy

    def tiles(n, body):
        def step(j, carry):
            body(pl.ds(pl.multiple_of(j * n, n), n))
            return carry

        lax.fori_loop(0, wide // n, step, 0)

    f32 = lambda a: a.astype(jnp.float32)
    bf16 = lambda a: a.astype(jnp.bfloat16)

    loads = [
        local(r["numer"], r["numer_v"]),
        local(r["ctx"], r["ctx_v"]),
        local(r["cot"], r["cots"].at[tp]),
        local(r["res"], r["res_v"]),
    ]
    weight = r["weight"][0]
    r["w_out"][...] = jnp.full(r["w_out"].shape, weight, jnp.float32)

    hops = sorted({hop for _, _, legs in pieces for hop in legs} | {1 << k})
    near = [at(over, tp), at(over, flip), at(rep, ahead), at(rep, behind)]
    near += [at((rep + sign * hop) % reps, tp) for hop in hops for sign in (1, -1)]
    barrier = pltpu.get_barrier_semaphore()
    for where in near:
        pl.semaphore_signal(barrier, inc=1, device_id=where, device_id_type=MESH)
    pl.semaphore_wait(barrier, len(near))

    a1 = send(r["cot"], r["y_relay"].at[0], at(over, tp))
    b_up = send(r["cot"], r["cots"].at[tp], at(rep, ahead))
    b_down = send(r["cot"], r["cots"].at[tp], at(rep, behind))

    arrived = {}

    def leg(p, i):
        row, rows, legs = pieces[p]
        where = at((rep + legs[i]) % reps, tp)
        span = pl.ds(row, rows)
        src = r["numer"].at[span] if i == 0 else r["legs"].at[i - 1, span]
        dst = r["peer_v"].at[span] if i == len(legs) - 1 else r["legs"].at[i, span]
        if i > 0:
            arrived[p].wait_recv()
        arrived[p] = send(src, dst, where)

    def legs_from(i):
        for p, (_, _, legs) in enumerate(pieces):
            if len(legs) > i:
                leg(p, i)

    for p in range(EARLY[k]):
        leg(p, 0)

    for copy in loads:
        copy.wait()
    r["ctx_t"][...] = r["ctx_v"][...].T

    def project(cols):
        params = bf16(f32(r["numer_v"][:, cols]) / weight)
        r["params"][:, cols] = params
        rows = jnp.dot(r["ctx_v"][...], params, preferred_element_type=jnp.float32)
        r["proj"][:, :, cols] = bf16(rows).reshape(tps, toks, WIDE)

    tiles(WIDE, project)
    w_copy = send(r["w_out"], r["w_in"], at((rep + (1 << k)) % reps, tp))

    far = (tp + tps // 2) % tps // 2 * 2
    up, down = ahead // 2 * 2, behind // 2 * 2
    e_up = send(r["proj"].at[far], r["part"].at[0], at(rep, ahead))
    e_down = send(r["proj"].at[far + 1], r["part"].at[1], at(rep, behind))
    a1.wait_recv()
    a2 = send(r["y_relay"].at[0], r["cots"].at[tp], at(over, flip))
    f_up = send(r["proj"].at[up + 1], r["sums"].at[1, 0], at(rep, ahead))
    f_down = send(r["proj"].at[down], r["sums"].at[0, 0], at(rep, behind))

    a2.wait_recv()
    c_up = send(r["cots"].at[flip], r["cots"].at[flip], at(rep, ahead))
    c_down = send(r["cots"].at[flip], r["cots"].at[flip], at(rep, behind))

    e_up.wait_recv()
    e_down.wait_recv()

    def join(cols):
        r["both"][0, :, cols] = bf16(f32(r["proj"][up, :, cols]) + f32(r["part"][0, :, cols]))
        r["both"][1, :, cols] = bf16(f32(r["proj"][down + 1, :, cols]) + f32(r["part"][1, :, cols]))

    tiles(FLAT, join)
    for copy in (b_up, b_down):
        copy.wait_recv()
    g_up = send(r["both"].at[0], r["sums"].at[0, 1], at(rep, ahead))
    g_down = send(r["both"].at[1], r["sums"].at[1, 1], at(rep, behind))

    c_up.wait_recv()
    c_down.wait_recv()
    d_up = send(r["cots"].at[down], r["cots"].at[down], at(rep, ahead))
    d_down = send(r["cots"].at[up + 1], r["cots"].at[up + 1], at(rep, behind))

    for copy in (f_up, f_down, g_up, g_down):
        copy.wait_recv()
    other = 1 - y_hi

    def total(cols):
        def of(half):
            mine = f32(r["proj"][x * 2 + half, :, cols])
            return mine + f32(r["sums"][half, 0, :, cols]) + f32(r["sums"][half, 1, :, cols])

        r["y_out"][:, cols] = bf16(of(other))
        r["own"][:, cols] = f32(r["res_v"][:, cols]) + of(y_hi)

    tiles(FLAT, total)
    legs_from(1)
    h1 = send(r["y_out"], r["y_relay"].at[1], at(over, tp))
    for p in range(EARLY[k], len(pieces)):
        leg(p, 0)

    d_up.wait_recv()
    d_down.wait_recv()
    h1.wait_recv()
    h2 = send(r["y_relay"].at[1], r["y_in"], at(over, flip))

    r["acc"][...] = jnp.zeros_like(r["acc"])

    def grads(cols):
        cot = r["cots"][:, :, cols].reshape(tps * toks, WIDE)
        slope = jnp.dot(r["ctx_t"][...], cot, preferred_element_type=jnp.float32)
        r["base"][:, cols] = 0.5 * f32(r["numer_v"][:, cols]) - LEARN * slope
        r["acc"][...] += lax.dot_general(
            cot, r["params"][:, cols], (((1,), (1,)), ((), ())), preferred_element_type=jnp.float32
        )

    tiles(WIDE, grads)
    r["ctx_v"][...] = bf16(r["acc"][...])
    stores = [local(r["ctx_v"], r["gctx"])]
    legs_from(2)

    h2.wait_recv()

    def finish(cols):
        r["res_v"][:, cols] = bf16(r["own"][:, cols] + f32(r["y_in"][:, cols]))

    tiles(FLAT, finish)
    stores.append(local(r["res_v"], r["out"]))
    w_copy.wait_recv()
    r["w_next"][0] = 0.5 * (weight + jnp.max(r["w_in"][...]))

    order = sorted(range(len(pieces)), key=lambda p: len(pieces[p][2]) > 1)
    for p in order:
        row, rows, _ = pieces[p]
        arrived[p].wait_recv()

        def mix(cols):
            value = r["base"][row : row + rows, cols] + 0.5 * f32(r["peer_v"][row : row + rows, cols])
            r["numer_v"][row : row + rows, cols] = bf16(value)

        tiles(FLAT, mix)
        stores.append(local(r["numer_v"].at[pl.ds(row, rows)], r["numer_next"].at[pl.ds(row, rows)]))

    for copy in stores:
        copy.wait()
    for copy in sends:
        copy.wait_send()


def step_at(k, reps, tps, context, residual, cotangent, numer, weight):
    toks, wide = residual.shape
    rows, feats = context.shape
    short, full = jnp.bfloat16, jnp.float32
    _, pieces = pieces_of(k)
    hops = sum(len(legs) for _, _, legs in pieces)
    n_legs = max(len(legs) for _, _, legs in pieces)
    leg_rows = sum(n for _, n, legs in pieces if len(legs) > 1)
    block = (toks, wide)
    hbm = pl.BlockSpec(memory_space=pl.ANY)
    smem = pl.BlockSpec(memory_space=pltpu.SMEM)
    scratch = {
        "numer_v": pltpu.VMEM((feats, wide), short),
        "params": pltpu.VMEM((feats, wide), short),
        "peer_v": pltpu.VMEM((feats, wide), short),
        "base": pltpu.VMEM((feats, wide), full),
        "legs": pltpu.VMEM((max(1, n_legs - 1), max(16, leg_rows), wide if leg_rows else 128), short),
        "ctx_v": pltpu.VMEM((rows, feats), short),
        "ctx_t": pltpu.VMEM((feats, rows), short),
        "acc": pltpu.VMEM((rows, feats), full),
        "cots": pltpu.VMEM((tps, *block), short),
        "proj": pltpu.VMEM((tps, *block), short),
        "part": pltpu.VMEM((2, *block), short),
        "both": pltpu.VMEM((2, *block), short),
        "sums": pltpu.VMEM((2, 2, *block), short),
        "y_relay": pltpu.VMEM((2, *block), short),
        "y_out": pltpu.VMEM(block, short),
        "y_in": pltpu.VMEM(block, short),
        "own": pltpu.VMEM(block, full),
        "res_v": pltpu.VMEM(block, short),
        "w_out": pltpu.VMEM((8, 128), full),
        "w_in": pltpu.VMEM((8, 128), full),
        "ss": pltpu.SemaphoreType.DMA((20 + hops,)),
        "rs": pltpu.SemaphoreType.DMA((20 + hops,)),
        "ls": pltpu.SemaphoreType.DMA((8 + len(pieces),)),
    }
    given = ("ctx", "res", "cot", "numer", "weight")
    made = ("out", "gctx", "numer_next", "w_next")
    return pl.pallas_call(
        functools.partial(kernel, k, reps, tps, (*given, *made, *scratch)),
        out_shape=(
            jax.ShapeDtypeStruct(residual.shape, short),
            jax.ShapeDtypeStruct(context.shape, short),
            jax.ShapeDtypeStruct(numer.shape, short),
            jax.ShapeDtypeStruct(weight.shape, full),
        ),
        in_specs=[hbm, hbm, hbm, hbm, smem],
        out_specs=(hbm, hbm, hbm, smem),
        scratch_shapes=list(scratch.values()),
        compiler_params=pltpu.CompilerParams(
            collective_id=k, has_side_effects=True, vmem_limit_bytes=63 * 2**20
        ),
        name=f"push_{k}",
    )(context, residual, cotangent, numer, weight)


def solution(mesh):
    reps, tps = mesh.shape["rep"], mesh.shape["tp"]
    both = P(("rep", "tp"), None)

    def on_device(context, residual, cotangent, numer, weight, step):
        k = jnp.remainder(step[0], jnp.int32(PEER_BITS + 1))
        branches = [functools.partial(step_at, bits, reps, tps) for bits in range(PEER_BITS + 1)]
        output, grad_ctx, numer_next, weight_next = lax.switch(
            k, branches, context, residual, cotangent, numer[0], weight
        )
        return output, grad_ctx, numer_next[None], weight_next

    return jax.shard_map(
        on_device,
        mesh=mesh,
        in_specs=(P("rep", "tp"), both, both, P("rep", "tp", None), P("rep"), P()),
        out_specs=(both, P("rep", "tp"), P("rep", "tp", None), P("rep")),
        check_vma=False,
    )
```

```python
import functools

import jax
import jax.numpy as jnp
from jax import lax
from jax.experimental import pallas as pl
from jax.experimental.pallas import tpu as pltpu
from jax.sharding import PartitionSpec as P

PEER_BITS = 3
LEARN = 0.001
MESH = pl.DeviceIdType.MESH
WIDE = 256
FLAT = 512

PLANS = (
    (((1,), (256, 64, 32, 32)),),
    (((2,), (192, 64, 64, 32, 32)),),
    (((-12, -12, -4), (16,) * 2), ((4,), (32,) * 11)),
    (((-12, -12), (16,) * 6), ((8,), (32,) * 9)),
)
WINDOW = 3


def legs(leg, *pieces):
    return tuple((p, leg) for p in pieces)


STARTS = (
    {"entry": legs(0, 0), "total": legs(0, 1), "relay": legs(0, 2, 3)},
    {"entry": legs(0, 0), "relay": legs(0, 1), "grads": legs(0, 2)},
    {
        "entry": legs(0, 0, 1, 2, 3, 4),
        "project": legs(0, 5),
        "join": legs(0, 6),
        "total": legs(1, 0, 1) + legs(0, 7),
        "relay": legs(0, 8, 9),
        "grads": legs(0, 10),
        "mix": legs(2, 0, 1),
    },
    {
        "entry": legs(0, 0, 1, 2, 6, 7, 8),
        "join": legs(0, 3, 4, 5),
        "total": legs(0, 9),
        "relay": legs(0, 10),
        "grads": legs(1, 0, 1, 2) + legs(0, 11),
        "mix4": legs(1, 3, 4, 5),
    },
)


def pieces_of(k):
    row, pieces = 0, []
    for offsets, sizes in PLANS[k]:
        for rows in sizes:
            pieces.append((row, rows, offsets))
            row += rows
    return row, pieces


def kernel(k, reps, tps, names, *refs):
    r = dict(zip(names, refs, strict=True))
    rep, tp = lax.axis_index("rep"), lax.axis_index("tp")
    x, y_hi = tp // 2, tp % 2
    over = rep + 2 - 4 * ((rep // 2) % 2)
    flip = tp + 1 - 2 * y_hi
    ahead, behind = (tp + 2) % tps, (tp + tps - 2) % tps
    at = lambda a, b: {"rep": a, "tp": b}
    _, pieces = pieces_of(k)
    feats, wide = r["numer"].shape
    toks = r["cot"].shape[0]

    used = {"s": 0, "r": 0}
    sends = []

    def send(src, dst, where):
        i = used["s"]
        used["s"] += 1
        copy = pltpu.make_async_remote_copy(
            src_ref=src,
            dst_ref=dst,
            send_sem=r["ss"].at[i],
            recv_sem=r["rs"].at[i],
            device_id=where,
            device_id_type=MESH,
        )
        copy.start()
        sends.append(copy)
        return copy

    def local(src, dst):
        i = used["r"]
        used["r"] += 1
        copy = pltpu.make_async_copy(src, dst, r["ls"].at[i])
        copy.start()
        return copy

    def tiles(n, body, part=0, parts=1):
        def step(j, carry):
            body(pl.ds(pl.multiple_of(j * n, n), n))
            return carry

        count = wide // n // parts
        lax.fori_loop(part * count, (part + 1) * count, step, 0)

    f32 = lambda a: a.astype(jnp.float32)
    bf16 = lambda a: a.astype(jnp.bfloat16)

    loads = [
        local(r["numer"], r["numer_v"]),
        local(r["ctx"], r["ctx_v"]),
        local(r["cot"], r["cots"].at[tp]),
        local(r["res"], r["res_v"]),
    ]
    weight = r["weight"][0]
    r["w_out"][...] = jnp.full(r["w_out"].shape, weight, jnp.float32)

    hops = sorted({hop for _, _, offsets in pieces for hop in offsets} | {1 << k})
    near = [at(over, tp), at(over, flip), at(rep, ahead), at(rep, behind)]
    near += [at((rep + sign * hop) % reps, tp) for hop in hops for sign in (1, -1)]
    barrier = pltpu.get_barrier_semaphore()
    for where in near:
        pl.semaphore_signal(barrier, inc=1, device_id=where, device_id_type=MESH)
    pl.semaphore_wait(barrier, len(near))

    halves = [pl.ds(i * toks // 2, toks // 2) for i in range(2)]
    a1 = [send(r["cot"].at[half], r["y_relay"].at[0, half], at(over, tp)) for half in halves]
    b_up = send(r["cot"], r["cots"].at[tp], at(rep, ahead))
    b_down = send(r["cot"], r["cots"].at[tp], at(rep, behind))

    arrived = {}

    def leg(p, i):
        row, rows, offsets = pieces[p]
        where = at((rep + offsets[i]) % reps, tp)
        span = pl.ds(row, rows)
        src = r["numer"].at[span] if i == 0 else r["legs"].at[i - 1, span]
        dst = r["peer_v"].at[span] if i == len(offsets) - 1 else r["legs"].at[i, span]
        if i > 0:
            arrived[p].wait_recv()
        arrived[p] = send(src, dst, where)

    def start_at(point):
        for p, i in STARTS[k].get(point, ()):
            leg(p, i)

    start_at("entry")

    for copy in loads:
        copy.wait()
    r["ctx_t"][...] = r["ctx_v"][...].T

    def project(cols):
        params = bf16(f32(r["numer_v"][:, cols]) / weight)
        r["params"][:, cols] = params
        rows = jnp.dot(r["ctx_v"][...], params, preferred_element_type=jnp.float32)
        r["proj"][:, :, cols] = bf16(rows).reshape(tps, toks, WIDE)

    far = (tp + tps // 2) % tps // 2 * 2
    up, down = ahead // 2 * 2, behind // 2 * 2
    parts = [pl.ds(i * wide // 2, wide // 2) for i in range(2)]

    e_up, e_down, g_up, g_down = [], [], [], []
    for i, part in enumerate(parts):
        tiles(WIDE, project, i, 2)
        e_up.append(send(r["proj"].at[far, :, part], r["part"].at[0, :, part], at(rep, ahead)))
        e_down.append(send(r["proj"].at[far + 1, :, part], r["part"].at[1, :, part], at(rep, behind)))
    w_copy = send(r["w_out"], r["w_in"], at((rep + (1 << k)) % reps, tp))
    start_at("project")
    a2 = []
    for copy, half in zip(a1, halves):
        copy.wait_recv()
        a2.append(send(r["y_relay"].at[0, half], r["cots"].at[tp, half], at(over, flip)))

    def join(cols):
        r["both"][0, :, cols] = bf16(f32(r["proj"][up, :, cols]) + f32(r["part"][0, :, cols]))
        r["both"][1, :, cols] = bf16(f32(r["proj"][down + 1, :, cols]) + f32(r["part"][1, :, cols]))

    for i, part in enumerate(parts):
        e_up[i].wait_recv()
        e_down[i].wait_recv()
        tiles(FLAT, join, i, 2)
        g_up.append(send(r["both"].at[0, :, part], r["sums"].at[0, 1, :, part], at(rep, ahead)))
        g_down.append(send(r["both"].at[1, :, part], r["sums"].at[1, 1, :, part], at(rep, behind)))
    f_up = send(r["proj"].at[up + 1], r["sums"].at[1, 0], at(rep, ahead))
    f_down = send(r["proj"].at[down], r["sums"].at[0, 0], at(rep, behind))
    start_at("join")

    for copy in (*g_up, *g_down, f_up, f_down, *a2):
        copy.wait_recv()
    c_up = send(r["cots"].at[flip], r["cots"].at[flip], at(rep, ahead))
    c_down = send(r["cots"].at[flip], r["cots"].at[flip], at(rep, behind))
    other = 1 - y_hi

    def total(cols):
        def of(half):
            mine = f32(r["proj"][x * 2 + half, :, cols])
            return mine + f32(r["sums"][half, 0, :, cols]) + f32(r["sums"][half, 1, :, cols])

        r["y_out"][:, cols] = bf16(of(other))
        r["own"][:, cols] = f32(r["res_v"][:, cols]) + of(y_hi)

    tiles(FLAT, total)
    h1 = [send(r["y_out"].at[half], r["y_relay"].at[1, half], at(over, tp)) for half in halves]
    start_at("total")

    for copy in (b_up, b_down, c_up, c_down):
        copy.wait_recv()
    d_up = send(r["cots"].at[down], r["cots"].at[down], at(rep, ahead))
    d_down = send(r["cots"].at[up + 1], r["cots"].at[up + 1], at(rep, behind))
    h2 = []
    for copy, half in zip(h1, halves):
        copy.wait_recv()
        h2.append(send(r["y_relay"].at[1, half], r["y_in"].at[half], at(over, flip)))
    start_at("relay")
    d_up.wait_recv()
    d_down.wait_recv()
    start_at("grads")

    r["acc"][...] = jnp.zeros_like(r["acc"])

    def grads(cols):
        cot = r["cots"][:, :, cols].reshape(tps * toks, WIDE)
        slope = jnp.dot(r["ctx_t"][...], cot, preferred_element_type=jnp.float32)
        r["base"][:, cols] = 0.5 * f32(r["numer_v"][:, cols]) - LEARN * slope
        r["acc"][...] += lax.dot_general(
            cot, r["params"][:, cols], (((1,), (1,)), ((), ())), preferred_element_type=jnp.float32
        )

    tiles(WIDE, grads)
    r["gctx"][...] = bf16(r["acc"][...])

    for copy in h2:
        copy.wait_recv()

    def finish(cols):
        r["out"][:, cols] = bf16(r["own"][:, cols] + f32(r["y_in"][:, cols]))

    tiles(FLAT, finish)
    w_copy.wait_recv()
    r["w_next"][0] = 0.5 * (weight + jnp.max(r["w_in"][...]))

    start_at("mix")
    direct = [p for p in range(len(pieces)) if len(pieces[p][2]) == 1]
    relayed = [p for p in range(len(pieces)) if len(pieces[p][2]) > 1]
    for n, p in enumerate(direct + relayed):
        row, rows, _ = pieces[p]
        start_at(f"mix{n}")
        arrived[p].wait_recv()
        for later in direct[: n + WINDOW + 1]:
            if later not in arrived:
                leg(later, 0)

        def mix(cols):
            value = r["base"][row : row + rows, cols] + 0.5 * f32(r["peer_v"][row : row + rows, cols])
            r["numer_next"][row : row + rows, cols] = bf16(value)

        tiles(FLAT, mix)

    for copy in sends:
        copy.wait_send()


def step_at(k, reps, tps, context, residual, cotangent, numer, weight):
    toks, wide = residual.shape
    rows, feats = context.shape
    short, full = jnp.bfloat16, jnp.float32
    _, pieces = pieces_of(k)
    hops = sum(len(offsets) for _, _, offsets in pieces)
    n_legs = max(len(offsets) for _, _, offsets in pieces)
    leg_rows = sum(n for _, n, offsets in pieces if len(offsets) > 1)
    block = (toks, wide)
    hbm = pl.BlockSpec(memory_space=pl.ANY)
    smem = pl.BlockSpec(memory_space=pltpu.SMEM)
    vmem = pl.BlockSpec(memory_space=pltpu.VMEM)
    scratch = {
        "numer_v": pltpu.VMEM((feats, wide), short),
        "params": pltpu.VMEM((feats, wide), short),
        "peer_v": pltpu.VMEM((feats, wide), short),
        "base": pltpu.VMEM((feats, wide), full),
        "legs": pltpu.VMEM((max(1, n_legs - 1), max(16, leg_rows), wide if leg_rows else 128), short),
        "ctx_v": pltpu.VMEM((rows, feats), short),
        "ctx_t": pltpu.VMEM((feats, rows), short),
        "acc": pltpu.VMEM((rows, feats), full),
        "cots": pltpu.VMEM((tps, *block), short),
        "proj": pltpu.VMEM((tps, *block), short),
        "part": pltpu.VMEM((2, *block), short),
        "both": pltpu.VMEM((2, *block), short),
        "sums": pltpu.VMEM((2, 2, *block), short),
        "y_relay": pltpu.VMEM((2, *block), short),
        "y_out": pltpu.VMEM(block, short),
        "y_in": pltpu.VMEM(block, short),
        "own": pltpu.VMEM(block, full),
        "res_v": pltpu.VMEM(block, short),
        "w_out": pltpu.VMEM((8, 128), full),
        "w_in": pltpu.VMEM((8, 128), full),
        "ss": pltpu.SemaphoreType.DMA((26 + hops,)),
        "rs": pltpu.SemaphoreType.DMA((26 + hops,)),
        "ls": pltpu.SemaphoreType.DMA((4,)),
    }
    given = ("ctx", "res", "cot", "numer", "weight")
    made = ("out", "gctx", "numer_next", "w_next")
    return pl.pallas_call(
        functools.partial(kernel, k, reps, tps, (*given, *made, *scratch)),
        out_shape=(
            jax.ShapeDtypeStruct(residual.shape, short),
            jax.ShapeDtypeStruct(context.shape, short),
            jax.ShapeDtypeStruct(numer.shape, short),
            jax.ShapeDtypeStruct(weight.shape, full),
        ),
        in_specs=[hbm, hbm, hbm, hbm, smem],
        out_specs=(vmem, vmem, vmem, smem),
        scratch_shapes=list(scratch.values()),
        compiler_params=pltpu.CompilerParams(
            collective_id=k, has_side_effects=True, vmem_limit_bytes=48 * 2**20
        ),
        name=f"push_{k}",
    )(context, residual, cotangent, numer, weight)


def solution(mesh):
    reps, tps = mesh.shape["rep"], mesh.shape["tp"]
    both = P(("rep", "tp"), None)

    def on_device(context, residual, cotangent, numer, weight, step):
        k = jnp.remainder(step[0], jnp.int32(PEER_BITS + 1))
        branches = [functools.partial(step_at, bits, reps, tps) for bits in range(PEER_BITS + 1)]
        output, grad_ctx, numer_next, weight_next = lax.switch(
            k, branches, context, residual, cotangent, numer[0], weight
        )
        return output, grad_ctx, numer_next[None], weight_next

    return jax.shard_map(
        on_device,
        mesh=mesh,
        in_specs=(P("rep", "tp"), both, both, P("rep", "tp", None), P("rep"), P()),
        out_specs=(both, P("rep", "tp"), P("rep", "tp", None), P("rep")),
        check_vma=False,
    )
```

```python
import functools

import jax
import jax.numpy as jnp
from jax import lax
from jax.experimental import pallas as pl
from jax.experimental.pallas import tpu as pltpu
from jax.sharding import PartitionSpec as P

PEER_BITS = 3
LEARN = 0.001
MESH = pl.DeviceIdType.MESH
WIDE = 256
FLAT = 512

GROUP = 4
PLANS = (
    (((1, GROUP), (96, 96, 64)), ((1,), (64, 48, 16))),
    (((2, GROUP), (64, 64)), ((2,), (64, 64, 48, 32, 32, 16))),
    (((-12, -12, -4), (16,) * 2), ((4,), (32,) * 10 + (16,) * 2)),
    (((-12, -12), (16,) * 6), ((8,), (32,) * 8 + (16,) * 2)),
)
WINDOW = 3


def legs(leg, *pieces):
    return tuple((p, leg) for p in pieces)


STARTS = (
    {
        "entry": legs(0, 0, 1, 2),
        "join": legs(1, 0),
        "total": legs(0, 3, 4, 5) + legs(1, 1, 2),
    },
    {
        "entry": legs(0, 0, 1),
        "join": legs(1, 0),
        "total": legs(0, 2, 3, 4, 5, 6, 7) + legs(1, 1),
    },
    {
        "entry": legs(0, 0, 1, 2, 3, 4, 5),
        "project": legs(0, 6),
        "join": legs(0, 7),
        "total": legs(1, 0, 1) + legs(0, 8),
        "relay": legs(0, 9, 10),
        "grads": legs(0, 11),
        "mix": legs(2, 0, 1),
    },
    {
        "entry": legs(0, 0, 1, 2, 6, 7, 8, 9),
        "join": legs(0, 3, 4, 5),
        "total": legs(0, 10),
        "relay": legs(0, 11),
        "grads": legs(1, 0, 1, 2) + legs(0, 12),
        "mix4": legs(1, 3, 4, 5),
    },
)


def pieces_of(k):
    row, pieces = 0, []
    for offsets, sizes in PLANS[k]:
        for rows in sizes:
            pieces.append((row, rows, offsets))
            row += rows
    return row, pieces


def kernel(k, reps, tps, names, *refs):
    r = dict(zip(names, refs, strict=True))
    rep, tp = lax.axis_index("rep"), lax.axis_index("tp")
    x, y_hi = tp // 2, tp % 2
    over = rep + 2 - 4 * ((rep // 2) % 2)
    flip = tp + 1 - 2 * y_hi
    ahead, behind = (tp + 2) % tps, (tp + tps - 2) % tps
    at = lambda a, b: {"rep": a, "tp": b}
    _, pieces = pieces_of(k)
    feats, wide = r["numer"].shape
    toks = r["cot"].shape[0]

    used = {"s": 0, "r": 0}
    sends = []

    def remote(src, dst, where):
        i = used["s"]
        used["s"] += 1
        return pltpu.make_async_remote_copy(
            src_ref=src,
            dst_ref=dst,
            send_sem=r["ss"].at[i],
            recv_sem=r["rs"].at[i],
            device_id=where,
            device_id_type=MESH,
        )

    def send(src, dst, where):
        copy = remote(src, dst, where)
        copy.start()
        sends.append(copy)
        return copy

    def local(src, dst):
        i = used["r"]
        used["r"] += 1
        copy = pltpu.make_async_copy(src, dst, r["ls"].at[i])
        copy.start()
        return copy

    def tiles(n, body, part=0, parts=1):
        def step(j, carry):
            body(pl.ds(pl.multiple_of(j * n, n), n))
            return carry

        count = wide // n // parts
        lax.fori_loop(part * count, (part + 1) * count, step, 0)

    f32 = lambda a: a.astype(jnp.float32)
    bf16 = lambda a: a.astype(jnp.bfloat16)

    loads = [
        local(r["numer"], r["numer_v"]),
        local(r["ctx"], r["ctx_v"]),
        local(r["cot"], r["cots"].at[tp]),
        local(r["res"], r["res_v"]),
    ]
    weight = r["weight"][0]
    r["w_out"][...] = jnp.full(r["w_out"].shape, weight, jnp.float32)

    hops = sorted({hop for _, _, offsets in pieces for hop in offsets} | {1 << k})
    near = [at(over, tp), at(over, flip), at(rep, ahead), at(rep, behind)]
    near += [at((rep + sign * hop) % reps, tp) for hop in hops for sign in (1, -1)]
    grouped = 1 << k < GROUP
    place = rep % GROUP
    beside = rep - place + (place + (1 << k)) % GROUP
    passes = place < 1 << k
    if grouped:
        near += [at(beside, tp), at(rep - place + (place + GROUP - (1 << k)) % GROUP, tp)]
        near += [at((rep + sign * GROUP) % reps, tp) for sign in (1, -1)]
    barrier = pltpu.get_barrier_semaphore()
    for where in near:
        pl.semaphore_signal(barrier, inc=1, device_id=where, device_id_type=MESH)
    pl.semaphore_wait(barrier, len(near))

    halves = [pl.ds(i * toks // 2, toks // 2) for i in range(2)]
    a1 = [send(r["cot"].at[half], r["y_relay"].at[0, half], at(over, tp)) for half in halves]
    b_up = send(r["cot"], r["cots"].at[tp], at(rep, ahead))
    b_down = send(r["cot"], r["cots"].at[tp], at(rep, behind))

    arrived, passed = {}, {}

    def pass_on(p):
        row, rows, _ = pieces[p]
        span = pl.ds(row, rows)
        passed[p] = remote(r["peer_v"].at[0, span], r["peer_v"].at[1, span], at((rep + GROUP) % reps, tp))

        @pl.when(passes)
        def _():
            arrived[p].wait_recv()
            passed[p].start()

    def leg(p, i):
        row, rows, offsets = pieces[p]
        if grouped and i > 0:
            pass_on(p)
            return
        where = at(beside if grouped and len(offsets) > 1 else (rep + offsets[i]) % reps, tp)
        span = pl.ds(row, rows)
        src = r["numer"].at[span] if i == 0 else r["legs"].at[i - 1, span]
        dst = r["peer_v"].at[0, span] if grouped or i == len(offsets) - 1 else r["legs"].at[i, span]
        if i > 0:
            arrived[p].wait_recv()
        arrived[p] = send(src, dst, where)

    def start_at(point):
        for p, i in STARTS[k].get(point, ()):
            leg(p, i)

    start_at("entry")

    for copy in loads:
        copy.wait()
    r["ctx_t"][...] = r["ctx_v"][...].T

    def project(cols):
        params = bf16(f32(r["numer_v"][:, cols]) / weight)
        r["params"][:, cols] = params
        rows = jnp.dot(r["ctx_v"][...], params, preferred_element_type=jnp.float32)
        r["proj"][:, :, cols] = bf16(rows).reshape(tps, toks, WIDE)

    far = (tp + tps // 2) % tps // 2 * 2
    up, down = ahead // 2 * 2, behind // 2 * 2
    parts = [pl.ds(i * wide // 2, wide // 2) for i in range(2)]

    e_up, e_down, g_up, g_down = [], [], [], []
    for i, part in enumerate(parts):
        tiles(WIDE, project, i, 2)
        e_up.append(send(r["proj"].at[far, :, part], r["part"].at[0, :, part], at(rep, ahead)))
        e_down.append(send(r["proj"].at[far + 1, :, part], r["part"].at[1, :, part], at(rep, behind)))
    w_copy = send(r["w_out"], r["w_in"], at((rep + (1 << k)) % reps, tp))
    start_at("project")
    a2 = []
    for copy, half in zip(a1, halves):
        copy.wait_recv()
        a2.append(send(r["y_relay"].at[0, half], r["cots"].at[tp, half], at(over, flip)))

    def join(cols):
        r["both"][0, :, cols] = bf16(f32(r["proj"][up, :, cols]) + f32(r["part"][0, :, cols]))
        r["both"][1, :, cols] = bf16(f32(r["proj"][down + 1, :, cols]) + f32(r["part"][1, :, cols]))

    for i, part in enumerate(parts):
        e_up[i].wait_recv()
        e_down[i].wait_recv()
        tiles(FLAT, join, i, 2)
        g_up.append(send(r["both"].at[0, :, part], r["sums"].at[0, 1, :, part], at(rep, ahead)))
        g_down.append(send(r["both"].at[1, :, part], r["sums"].at[1, 1, :, part], at(rep, behind)))
    f_up = send(r["proj"].at[up + 1], r["sums"].at[1, 0], at(rep, ahead))
    f_down = send(r["proj"].at[down], r["sums"].at[0, 0], at(rep, behind))
    start_at("join")

    for copy in (*g_up, *g_down, f_up, f_down, *a2):
        copy.wait_recv()
    c_up = send(r["cots"].at[flip], r["cots"].at[flip], at(rep, ahead))
    c_down = send(r["cots"].at[flip], r["cots"].at[flip], at(rep, behind))
    other = 1 - y_hi

    def total(cols):
        def of(half):
            mine = f32(r["proj"][x * 2 + half, :, cols])
            return mine + f32(r["sums"][half, 0, :, cols]) + f32(r["sums"][half, 1, :, cols])

        r["y_out"][:, cols] = bf16(of(other))
        r["own"][:, cols] = f32(r["res_v"][:, cols]) + of(y_hi)

    tiles(FLAT, total)
    h1 = [send(r["y_out"].at[half], r["y_relay"].at[1, half], at(over, tp)) for half in halves]
    start_at("total")

    for copy in (b_up, b_down, c_up, c_down):
        copy.wait_recv()
    d_up = send(r["cots"].at[down], r["cots"].at[down], at(rep, ahead))
    d_down = send(r["cots"].at[up + 1], r["cots"].at[up + 1], at(rep, behind))
    h2 = []
    for copy, half in zip(h1, halves):
        copy.wait_recv()
        h2.append(send(r["y_relay"].at[1, half], r["y_in"].at[half], at(over, flip)))
    start_at("relay")
    d_up.wait_recv()
    d_down.wait_recv()
    start_at("grads")

    r["acc"][...] = jnp.zeros_like(r["acc"])

    def grads(cols):
        cot = r["cots"][:, :, cols].reshape(tps * toks, WIDE)
        slope = jnp.dot(r["ctx_t"][...], cot, preferred_element_type=jnp.float32)
        r["base"][:, cols] = 0.5 * f32(r["numer_v"][:, cols]) - LEARN * slope
        r["acc"][...] += lax.dot_general(
            cot, r["params"][:, cols], (((1,), (1,)), ((), ())), preferred_element_type=jnp.float32
        )

    tiles(WIDE, grads)
    r["gctx"][...] = bf16(r["acc"][...])

    for copy in h2:
        copy.wait_recv()

    def finish(cols):
        r["out"][:, cols] = bf16(r["own"][:, cols] + f32(r["y_in"][:, cols]))

    tiles(FLAT, finish)
    w_copy.wait_recv()
    r["w_next"][0] = 0.5 * (weight + jnp.max(r["w_in"][...]))

    start_at("mix")
    direct = [p for p in range(len(pieces)) if len(pieces[p][2]) == 1]
    relayed = [p for p in range(len(pieces)) if len(pieces[p][2]) > 1]
    def mix_piece(p):
        row, rows, _ = pieces[p]
        half = 0
        if p in passed:
            half = jnp.where(passes, 1, 0)
            pl.when(passes)(passed[p].wait_recv)
            pl.when(jnp.logical_not(passes))(arrived[p].wait_recv)
        else:
            arrived[p].wait_recv()

        def mix(cols):
            value = r["base"][row : row + rows, cols] + 0.5 * f32(r["peer_v"][half, row : row + rows, cols])
            r["numer_next"][row : row + rows, cols] = bf16(value)

        tiles(FLAT, mix)

    for n, p in enumerate(range(len(pieces)) if grouped else direct + relayed):
        start_at(f"mix{n}")
        mix_piece(p)
        for later in direct[: n + WINDOW + 1]:
            if later not in arrived:
                leg(later, 0)

    for copy in sends:
        copy.wait_send()
    for copy in passed.values():
        pl.when(passes)(copy.wait_send)


def step_at(k, reps, tps, context, residual, cotangent, numer, weight):
    toks, wide = residual.shape
    rows, feats = context.shape
    short, full = jnp.bfloat16, jnp.float32
    _, pieces = pieces_of(k)
    hops = sum(len(offsets) for _, _, offsets in pieces)
    n_legs = max(len(offsets) for _, _, offsets in pieces)
    leg_rows = 0 if 1 << k < GROUP else sum(n for _, n, offsets in pieces if len(offsets) > 1)
    block = (toks, wide)
    hbm = pl.BlockSpec(memory_space=pl.ANY)
    smem = pl.BlockSpec(memory_space=pltpu.SMEM)
    vmem = pl.BlockSpec(memory_space=pltpu.VMEM)
    scratch = {
        "numer_v": pltpu.VMEM((feats, wide), short),
        "params": pltpu.VMEM((feats, wide), short),
        "peer_v": pltpu.VMEM((2 if 1 << k < GROUP else 1, feats, wide), short),
        "base": pltpu.VMEM((feats, wide), full),
        "legs": pltpu.VMEM((max(1, n_legs - 1), max(16, leg_rows), wide if leg_rows else 128), short),
        "ctx_v": pltpu.VMEM((rows, feats), short),
        "ctx_t": pltpu.VMEM((feats, rows), short),
        "acc": pltpu.VMEM((rows, feats), full),
        "cots": pltpu.VMEM((tps, *block), short),
        "proj": pltpu.VMEM((tps, *block), short),
        "part": pltpu.VMEM((2, *block), short),
        "both": pltpu.VMEM((2, *block), short),
        "sums": pltpu.VMEM((2, 2, *block), short),
        "y_relay": pltpu.VMEM((2, *block), short),
        "y_out": pltpu.VMEM(block, short),
        "y_in": pltpu.VMEM(block, short),
        "own": pltpu.VMEM(block, full),
        "res_v": pltpu.VMEM(block, short),
        "w_out": pltpu.VMEM((8, 128), full),
        "w_in": pltpu.VMEM((8, 128), full),
        "ss": pltpu.SemaphoreType.DMA((26 + hops + len(pieces),)),
        "rs": pltpu.SemaphoreType.DMA((26 + hops + len(pieces),)),
        "ls": pltpu.SemaphoreType.DMA((4,)),
    }
    given = ("ctx", "res", "cot", "numer", "weight")
    made = ("out", "gctx", "numer_next", "w_next")
    return pl.pallas_call(
        functools.partial(kernel, k, reps, tps, (*given, *made, *scratch)),
        out_shape=(
            jax.ShapeDtypeStruct(residual.shape, short),
            jax.ShapeDtypeStruct(context.shape, short),
            jax.ShapeDtypeStruct(numer.shape, short),
            jax.ShapeDtypeStruct(weight.shape, full),
        ),
        in_specs=[hbm, hbm, hbm, hbm, smem],
        out_specs=(vmem, vmem, vmem, smem),
        scratch_shapes=list(scratch.values()),
        compiler_params=pltpu.CompilerParams(
            collective_id=k, has_side_effects=True, vmem_limit_bytes=48 * 2**20
        ),
        name=f"push_{k}",
    )(context, residual, cotangent, numer, weight)


def solution(mesh):
    reps, tps = mesh.shape["rep"], mesh.shape["tp"]
    both = P(("rep", "tp"), None)

    def on_device(context, residual, cotangent, numer, weight, step):
        k = jnp.remainder(step[0], jnp.int32(PEER_BITS + 1))
        branches = [functools.partial(step_at, bits, reps, tps) for bits in range(PEER_BITS + 1)]
        output, grad_ctx, numer_next, weight_next = lax.switch(
            k, branches, context, residual, cotangent, numer[0], weight
        )
        return output, grad_ctx, numer_next[None], weight_next

    return jax.shard_map(
        on_device,
        mesh=mesh,
        in_specs=(P("rep", "tp"), both, both, P("rep", "tp", None), P("rep"), P()),
        out_specs=(both, P("rep", "tp"), P("rep", "tp", None), P("rep")),
        check_vma=False,
    )
```

```python
import functools

import jax
import jax.numpy as jnp
from jax import lax
from jax.experimental import pallas as pl
from jax.experimental.pallas import tpu as pltpu
from jax.sharding import PartitionSpec as P

PEER_BITS = 3
LEARN = 0.001
MESH = pl.DeviceIdType.MESH
WIDE = 256
FLAT = 512

GROUP = 4
PLANS = (
    (((1, GROUP), (96, 96, 64)), ((1,), (64, 48, 16))),
    (((2, GROUP), (64, 64)), ((2,), (64, 64, 48, 32, 32, 16))),
    (((-12, -12, -4), (16,) * 3), ((4,), (32,) * 10 + (16,))),
    (((-12, -12), (16,) * 6), ((8,), (32,) * 8 + (16,) * 2)),
)
WINDOW = 3


def legs(leg, *pieces):
    return tuple((p, leg) for p in pieces)


STARTS = (
    {
        "entry": legs(0, 0, 1, 2),
        "join": legs(1, 0),
        "total": legs(0, 3, 4, 5) + legs(1, 1, 2),
    },
    {
        "entry": legs(0, 0, 1),
        "join": legs(1, 0),
        "total": legs(0, 2, 3, 4, 5, 6, 7) + legs(1, 1),
    },
    {
        "entry": legs(0, 0, 1, 2, 3, 4, 5, 6),
        "project": legs(0, 7),
        "join": legs(0, 8),
        "total": legs(1, 0, 1, 2) + legs(0, 9),
        "relay": legs(0, 10, 11),
        "grads": legs(0, 12),
        "mix3": legs(2, 0, 1, 2),
    },
    {
        "entry": legs(0, 0, 1, 2, 6, 7, 8, 9),
        "join": legs(0, 3, 4, 5),
        "total": legs(0, 10),
        "relay": legs(0, 11),
        "grads": legs(1, 0, 1, 2) + legs(0, 12),
        "mix4": legs(1, 3, 4, 5),
    },
)


def pieces_of(k):
    row, pieces = 0, []
    for offsets, sizes in PLANS[k]:
        for rows in sizes:
            pieces.append((row, rows, offsets))
            row += rows
    return row, pieces


def kernel(k, reps, tps, names, *refs):
    r = dict(zip(names, refs, strict=True))
    rep, tp = lax.axis_index("rep"), lax.axis_index("tp")
    x, y_hi = tp // 2, tp % 2
    over = rep + 2 - 4 * ((rep // 2) % 2)
    flip = tp + 1 - 2 * y_hi
    ahead, behind = (tp + 2) % tps, (tp + tps - 2) % tps
    at = lambda a, b: {"rep": a, "tp": b}
    _, pieces = pieces_of(k)
    feats, wide = r["numer"].shape
    toks = r["cot"].shape[0]

    used = {"s": 0, "r": 0}
    sends = []

    def remote(src, dst, where):
        i = used["s"]
        used["s"] += 1
        return pltpu.make_async_remote_copy(
            src_ref=src,
            dst_ref=dst,
            send_sem=r["ss"].at[i],
            recv_sem=r["rs"].at[i],
            device_id=where,
            device_id_type=MESH,
        )

    def send(src, dst, where):
        copy = remote(src, dst, where)
        copy.start()
        sends.append(copy)
        return copy

    def local(src, dst):
        i = used["r"]
        used["r"] += 1
        copy = pltpu.make_async_copy(src, dst, r["ls"].at[i])
        copy.start()
        return copy

    def tiles(n, body, part=0, parts=1):
        def step(j, carry):
            body(pl.ds(pl.multiple_of(j * n, n), n))
            return carry

        count = wide // n // parts
        lax.fori_loop(part * count, (part + 1) * count, step, 0)

    f32 = lambda a: a.astype(jnp.float32)
    bf16 = lambda a: a.astype(jnp.bfloat16)

    loads = [
        local(r["numer"], r["numer_v"]),
        local(r["ctx"], r["ctx_v"]),
        local(r["cot"], r["cots"].at[tp]),
        local(r["res"], r["res_v"]),
    ]
    weight = r["weight"][0]
    r["w_out"][...] = jnp.full(r["w_out"].shape, weight, jnp.float32)

    hops = sorted({hop for _, _, offsets in pieces for hop in offsets} | {1 << k})
    near = [at(over, tp), at(over, flip), at(rep, ahead), at(rep, behind)]
    near += [at((rep + sign * hop) % reps, tp) for hop in hops for sign in (1, -1)]
    grouped = 1 << k < GROUP
    place = rep % GROUP
    beside = rep - place + (place + (1 << k)) % GROUP
    passes = place < 1 << k
    if grouped:
        near += [at(beside, tp), at(rep - place + (place + GROUP - (1 << k)) % GROUP, tp)]
        near += [at((rep + sign * GROUP) % reps, tp) for sign in (1, -1)]
    barrier = pltpu.get_barrier_semaphore()
    for where in near:
        pl.semaphore_signal(barrier, inc=1, device_id=where, device_id_type=MESH)
    pl.semaphore_wait(barrier, len(near))

    halves = [pl.ds(i * toks // 2, toks // 2) for i in range(2)]
    a1 = [send(r["cot"].at[half], r["y_relay"].at[0, half], at(over, tp)) for half in halves]
    b_up = send(r["cot"], r["cots"].at[tp], at(rep, ahead))
    b_down = send(r["cot"], r["cots"].at[tp], at(rep, behind))

    arrived, passed = {}, {}

    def pass_on(p):
        row, rows, _ = pieces[p]
        span = pl.ds(row, rows)
        passed[p] = remote(r["peer_v"].at[0, span], r["peer_v"].at[1, span], at((rep + GROUP) % reps, tp))

        @pl.when(passes)
        def _():
            arrived[p].wait_recv()
            passed[p].start()

    def leg(p, i):
        row, rows, offsets = pieces[p]
        if grouped and i > 0:
            pass_on(p)
            return
        where = at(beside if grouped and len(offsets) > 1 else (rep + offsets[i]) % reps, tp)
        span = pl.ds(row, rows)
        src = r["numer"].at[span] if i == 0 else r["legs"].at[i - 1, span]
        dst = r["peer_v"].at[0, span] if grouped or i == len(offsets) - 1 else r["legs"].at[i, span]
        if i > 0:
            arrived[p].wait_recv()
        arrived[p] = send(src, dst, where)

    def start_at(point):
        for p, i in STARTS[k].get(point, ()):
            leg(p, i)

    start_at("entry")

    for copy in loads:
        copy.wait()
    r["ctx_t"][...] = r["ctx_v"][...].T

    def project(cols):
        params = bf16(f32(r["numer_v"][:, cols]) / weight)
        r["params"][:, cols] = params
        rows = jnp.dot(r["ctx_v"][...], params, preferred_element_type=jnp.float32)
        r["proj"][:, :, cols] = bf16(rows).reshape(tps, toks, WIDE)

    far = (tp + tps // 2) % tps // 2 * 2
    up, down = ahead // 2 * 2, behind // 2 * 2
    parts = [pl.ds(i * wide // 2, wide // 2) for i in range(2)]

    e_up, e_down, g_up, g_down = [], [], [], []
    for i, part in enumerate(parts):
        tiles(WIDE, project, i, 2)
        e_up.append(send(r["proj"].at[far, :, part], r["part"].at[0, :, part], at(rep, ahead)))
        e_down.append(send(r["proj"].at[far + 1, :, part], r["part"].at[1, :, part], at(rep, behind)))
    w_copy = send(r["w_out"], r["w_in"], at((rep + (1 << k)) % reps, tp))
    start_at("project")
    a2 = []
    for copy, half in zip(a1, halves):
        copy.wait_recv()
        a2.append(send(r["y_relay"].at[0, half], r["cots"].at[tp, half], at(over, flip)))

    def join(cols):
        r["both"][0, :, cols] = bf16(f32(r["proj"][up, :, cols]) + f32(r["part"][0, :, cols]))
        r["both"][1, :, cols] = bf16(f32(r["proj"][down + 1, :, cols]) + f32(r["part"][1, :, cols]))

    for i, part in enumerate(parts):
        e_up[i].wait_recv()
        e_down[i].wait_recv()
        tiles(FLAT, join, i, 2)
        g_up.append(send(r["both"].at[0, :, part], r["sums"].at[0, 1, :, part], at(rep, ahead)))
        g_down.append(send(r["both"].at[1, :, part], r["sums"].at[1, 1, :, part], at(rep, behind)))
    f_up = send(r["proj"].at[up + 1], r["sums"].at[1, 0], at(rep, ahead))
    f_down = send(r["proj"].at[down], r["sums"].at[0, 0], at(rep, behind))
    start_at("join")

    for copy in (*g_up, *g_down, f_up, f_down, *a2):
        copy.wait_recv()
    c_up = send(r["cots"].at[flip], r["cots"].at[flip], at(rep, ahead))
    c_down = send(r["cots"].at[flip], r["cots"].at[flip], at(rep, behind))
    other = 1 - y_hi

    def total(cols):
        def of(half):
            mine = f32(r["proj"][x * 2 + half, :, cols])
            return mine + f32(r["sums"][half, 0, :, cols]) + f32(r["sums"][half, 1, :, cols])

        r["y_out"][:, cols] = bf16(of(other))
        r["own"][:, cols] = f32(r["res_v"][:, cols]) + of(y_hi)

    tiles(FLAT, total)
    h1 = [send(r["y_out"].at[half], r["y_relay"].at[1, half], at(over, tp)) for half in halves]
    start_at("total")

    for copy in (b_up, b_down, c_up, c_down):
        copy.wait_recv()
    d_up = send(r["cots"].at[down], r["cots"].at[down], at(rep, ahead))
    d_down = send(r["cots"].at[up + 1], r["cots"].at[up + 1], at(rep, behind))
    h2 = []
    for copy, half in zip(h1, halves):
        copy.wait_recv()
        h2.append(send(r["y_relay"].at[1, half], r["y_in"].at[half], at(over, flip)))
    start_at("relay")
    d_up.wait_recv()
    d_down.wait_recv()
    start_at("grads")

    r["acc"][...] = jnp.zeros_like(r["acc"])

    def grads(cols):
        cot = r["cots"][:, :, cols].reshape(tps * toks, WIDE)
        slope = jnp.dot(r["ctx_t"][...], cot, preferred_element_type=jnp.float32)
        r["base"][:, cols] = 0.5 * f32(r["numer_v"][:, cols]) - LEARN * slope
        r["acc"][...] += lax.dot_general(
            cot, r["params"][:, cols], (((1,), (1,)), ((), ())), preferred_element_type=jnp.float32
        )

    tiles(WIDE, grads)
    r["gctx"][...] = bf16(r["acc"][...])

    for copy in h2:
        copy.wait_recv()

    def finish(cols):
        r["out"][:, cols] = bf16(r["own"][:, cols] + f32(r["y_in"][:, cols]))

    tiles(FLAT, finish)
    w_copy.wait_recv()
    r["w_next"][0] = 0.5 * (weight + jnp.max(r["w_in"][...]))

    start_at("mix")
    direct = [p for p in range(len(pieces)) if len(pieces[p][2]) == 1]
    relayed = [p for p in range(len(pieces)) if len(pieces[p][2]) > 1]
    def mix_piece(p):
        row, rows, _ = pieces[p]
        half = 0
        if p in passed:
            half = jnp.where(passes, 1, 0)
            pl.when(passes)(passed[p].wait_recv)
            pl.when(jnp.logical_not(passes))(arrived[p].wait_recv)
        else:
            arrived[p].wait_recv()

        def mix(cols):
            value = r["base"][row : row + rows, cols] + 0.5 * f32(r["peer_v"][half, row : row + rows, cols])
            r["numer_next"][row : row + rows, cols] = bf16(value)

        tiles(FLAT, mix)

    for n, p in enumerate(range(len(pieces)) if grouped else direct + relayed):
        start_at(f"mix{n}")
        mix_piece(p)
        for later in direct[: n + WINDOW + 1]:
            if later not in arrived:
                leg(later, 0)

    for copy in sends:
        copy.wait_send()
    for copy in passed.values():
        pl.when(passes)(copy.wait_send)


def step_at(k, reps, tps, context, residual, cotangent, numer, weight):
    toks, wide = residual.shape
    rows, feats = context.shape
    short, full = jnp.bfloat16, jnp.float32
    _, pieces = pieces_of(k)
    hops = sum(len(offsets) for _, _, offsets in pieces)
    n_legs = max(len(offsets) for _, _, offsets in pieces)
    leg_rows = 0 if 1 << k < GROUP else sum(n for _, n, offsets in pieces if len(offsets) > 1)
    block = (toks, wide)
    hbm = pl.BlockSpec(memory_space=pl.ANY)
    smem = pl.BlockSpec(memory_space=pltpu.SMEM)
    vmem = pl.BlockSpec(memory_space=pltpu.VMEM)
    scratch = {
        "numer_v": pltpu.VMEM((feats, wide), short),
        "params": pltpu.VMEM((feats, wide), short),
        "peer_v": pltpu.VMEM((2 if 1 << k < GROUP else 1, feats, wide), short),
        "base": pltpu.VMEM((feats, wide), full),
        "legs": pltpu.VMEM((max(1, n_legs - 1), max(16, leg_rows), wide if leg_rows else 128), short),
        "ctx_v": pltpu.VMEM((rows, feats), short),
        "ctx_t": pltpu.VMEM((feats, rows), short),
        "acc": pltpu.VMEM((rows, feats), full),
        "cots": pltpu.VMEM((tps, *block), short),
        "proj": pltpu.VMEM((tps, *block), short),
        "part": pltpu.VMEM((2, *block), short),
        "both": pltpu.VMEM((2, *block), short),
        "sums": pltpu.VMEM((2, 2, *block), short),
        "y_relay": pltpu.VMEM((2, *block), short),
        "y_out": pltpu.VMEM(block, short),
        "y_in": pltpu.VMEM(block, short),
        "own": pltpu.VMEM(block, full),
        "res_v": pltpu.VMEM(block, short),
        "w_out": pltpu.VMEM((8, 128), full),
        "w_in": pltpu.VMEM((8, 128), full),
        "ss": pltpu.SemaphoreType.DMA((26 + hops + len(pieces),)),
        "rs": pltpu.SemaphoreType.DMA((26 + hops + len(pieces),)),
        "ls": pltpu.SemaphoreType.DMA((4,)),
    }
    given = ("ctx", "res", "cot", "numer", "weight")
    made = ("out", "gctx", "numer_next", "w_next")
    return pl.pallas_call(
        functools.partial(kernel, k, reps, tps, (*given, *made, *scratch)),
        out_shape=(
            jax.ShapeDtypeStruct(residual.shape, short),
            jax.ShapeDtypeStruct(context.shape, short),
            jax.ShapeDtypeStruct(numer.shape, short),
            jax.ShapeDtypeStruct(weight.shape, full),
        ),
        in_specs=[hbm, hbm, hbm, hbm, smem],
        out_specs=(vmem, vmem, vmem, smem),
        scratch_shapes=list(scratch.values()),
        compiler_params=pltpu.CompilerParams(
            collective_id=k, has_side_effects=True, vmem_limit_bytes=48 * 2**20
        ),
        name=f"push_{k}",
    )(context, residual, cotangent, numer, weight)


def solution(mesh):
    reps, tps = mesh.shape["rep"], mesh.shape["tp"]
    both = P(("rep", "tp"), None)

    def on_device(context, residual, cotangent, numer, weight, step):
        k = jnp.remainder(step[0], jnp.int32(PEER_BITS + 1))
        branches = [functools.partial(step_at, bits, reps, tps) for bits in range(PEER_BITS + 1)]
        output, grad_ctx, numer_next, weight_next = lax.switch(
            k, branches, context, residual, cotangent, numer[0], weight
        )
        return output, grad_ctx, numer_next[None], weight_next

    return jax.shard_map(
        on_device,
        mesh=mesh,
        in_specs=(P("rep", "tp"), both, both, P("rep", "tp", None), P("rep"), P()),
        out_specs=(both, P("rep", "tp"), P("rep", "tp", None), P("rep")),
        check_vma=False,
    )
```
